32 devices in a mesh: grp: 2 (over x), kv: 16 (over z, y, core).
Axes of the slice: x: 2, y: 2, z: 4, core: 2. Of those that a mesh axis runs over, the one named last changes fastest.
Arguments:
- absorbed_query: bfloat16 [8, 128, 576], P('grp', 'kv'), parts along dimension 0, may hold values from -65 to 65
- latent_cache: bfloat16 [8, 32768, 576], P('grp', 'kv'), parts along dimension 0, may hold values from -6 to 6
- slot_position: int32 [8, 32768], P('grp', 'kv'), parts along dimension 0, may hold values from 0 to 32767, as said below
- context_lengths: int32 [8], P('grp'), parts along dimension 0, may hold values from 16384 to 32768, as said below
- value_up: bfloat16 [128, 512, 128], P('kv'), may hold values from -2.09375 to 2.09375
Outputs:
- attended: bfloat16 [8, 16384], P('grp', 'kv'), parts along dimension 0
The draws below stay inside these ranges and needn't reach their ends.
There are 2 independent parts, one for each index of `grp`. The reference program is written for one: setup_inputs(seed, part) draws one part's arguments, and reference() takes and returns one part's arrays. A program takes and returns all parts, laid end to end along the dimension named above; an argument that names none is the same for every part. Nothing has to cross between parts.
Inputs may be any that keep to these rules, and one draw needn't show every extreme that they name: `slot_position`: each row is an ordering of 0 to 32767. `context_lengths`: some request holds exactly 32768 tokens.
All inputs are finite; a program needn't handle non-finite values.
Results may differ from the reference program's by a relative error of at most 0.0095.
Values may be sent and summed in bfloat16 or wider, within the bound.
A program may use at most 64 MiB of HBM per device.

```python
import jax
import jax.numpy as jnp
from jax import lax

H = 128
DL = 512
VH = 128
REQ = 4
DQ = 576
SLOTS = 32768


def permuted_rows(key):
    row_keys = jax.random.split(jax.random.fold_in(key, 101), REQ)
    return jax.vmap(lambda row_key: jax.random.permutation(row_key, SLOTS))(row_keys).astype(jnp.int32)


def draw_absorbed_query(key, part):
    drawn = jnp.clip(jax.random.normal(jax.random.fold_in(key, 11), (REQ, H, DQ), jnp.float32), -6.0, 6.0) * 1.3
    return drawn.astype(jnp.bfloat16)


def draw_latent_cache(key, part):
    drawn = jnp.clip(jax.random.normal(jax.random.fold_in(key, 12), (REQ, SLOTS, DQ), jnp.float32), -6.0, 6.0)
    return drawn.astype(jnp.bfloat16)


def draw_slot_position(key, part):
    return permuted_rows(key)


def draw_context_lengths(key, part):
    drawn = jax.random.randint(jax.random.fold_in(key, 13), (REQ,), SLOTS // 2, SLOTS + 1).astype(jnp.int32)
    longest = jax.random.randint(jax.random.fold_in(key, 14), (), 0, REQ).astype(jnp.int32)
    return jnp.where(jnp.arange(REQ, dtype=jnp.int32) == longest, jnp.int32(SLOTS), drawn).astype(jnp.int32)


def block_scale(stream_key, extent, shards, smallest, top_value):
    loudness, own = 1.0, jax.random.fold_in(stream_key, 6)
    for dim, blocks in shards:
        heights = jnp.exp(jax.random.uniform(jax.random.fold_in(own, dim), (blocks,), jnp.float32, smallest / len(shards), top_value / len(shards)))
        loudness = loudness * jnp.repeat(heights, extent[dim] // blocks).reshape([-1 if axis == dim else 1 for axis in range(len(extent))])
    return loudness


def normal_values(stream_key, dims, spread, bound, pieces=(), held_as=jnp.bfloat16):
    entries = spread * jax.random.normal(stream_key, dims, jnp.float32)
    if pieces:
        entries = entries * block_scale(stream_key, dims, pieces, -0.22, 0.18)
    return jnp.clip(entries, -bound, bound).astype(held_as)


def setup_inputs(seed: int = 0, part: int = 0) -> dict:
    splits = jax.random.split(jax.random.key(seed), 6)
    part_splits = jax.random.split(jax.random.fold_in(splits[5], part), 6)
    return {
        "absorbed_query": draw_absorbed_query(jax.random.fold_in(jax.random.fold_in(splits[5], part), 71), part),
        "latent_cache": draw_latent_cache(jax.random.fold_in(jax.random.fold_in(splits[5], part), 71), part),
        "slot_position": draw_slot_position(jax.random.fold_in(jax.random.fold_in(splits[5], part), 71), part),
        "context_lengths": draw_context_lengths(jax.random.fold_in(jax.random.fold_in(splits[5], part), 71), part),
        "value_up": normal_values(splits[4], (H, DL, VH), 0.35, 2.09375, ((0, 16),)),
    }


softmax_scale = 192.0 ** -0.5
masked_score = -1.0e30


def request_output(request_item, value_up):
    query_rows, cache_rows, positions, length = request_item
    scores = jnp.dot(query_rows, cache_rows.T, preferred_element_type=jnp.float32) * softmax_scale
    usable = (positions < length)[None, :]
    row_peak = jnp.max(jnp.where(usable, scores, masked_score), axis=1, keepdims=True)
    weights = jnp.where(usable, jnp.exp(scores - row_peak), jnp.float32(0.0))
    row_total = jnp.sum(weights, axis=1, keepdims=True)
    mixed_sum = jnp.dot(weights.astype(jnp.bfloat16), cache_rows[:, :DL], preferred_element_type=jnp.float32)
    latent_out = (mixed_sum / row_total).astype(jnp.bfloat16)
    projected = jnp.einsum("hl,hlv->hv", latent_out.astype(jnp.float32), value_up.astype(jnp.float32))
    return projected.astype(jnp.bfloat16).reshape(H * VH)


def reference(absorbed_query, latent_cache, slot_position, context_lengths, value_up):
    def per_request(request_item):
        return request_output(request_item, value_up)

    return lax.map(per_request, (absorbed_query, latent_cache, slot_position, context_lengths))
```

```python
import functools

import jax
import jax.numpy as jnp
from jax import lax
from jax.experimental import pallas as pl
from jax.experimental.pallas import tpu as pltpu
from jax.sharding import PartitionSpec as P

softmax_scale = 192.0 ** (-0.5)
masked_score = -1e30
MESH = pl.DeviceIdType.MESH
LANES = 128


def merge(parts):
    peak = functools.reduce(jnp.maximum, [lse for _, lse in parts])
    factors = [jnp.exp(lse - peak) for _, lse in parts]
    total = sum(factors[1:], factors[0])
    inverse = 1.0 / total
    mixed = sum(
        [part * (f * inverse) for (part, _), f in zip(parts[1:], factors[1:])],
        parts[0][0] * (factors[0] * inverse),
    )
    return mixed, peak + jnp.log(total)


def packed(mixed, lse):
    lanes = lax.broadcasted_iota(jnp.int32, (mixed.shape[0], LANES), 1)
    high = lse.astype(jnp.bfloat16).astype(jnp.float32)
    rest = lse - high
    middle = rest.astype(jnp.bfloat16).astype(jnp.float32)
    low = rest - middle
    return mixed.astype(jnp.bfloat16), jnp.where(
        lanes == 0, high, jnp.where(lanes == 1, middle, low)
    ).astype(jnp.bfloat16)


def unpacked(ref, latent):
    mixed = ref[:, :latent].astype(jnp.float32)
    tail = ref[:, latent:].astype(jnp.float32)
    return mixed, (tail[:, 0:1] + tail[:, 1:2]) + tail[:, 2:3]


def kernel(
    depth, q_ref, k_hbm, pos_ref, len_ref, w_hbm, out_ref,
    kbuf, wbuf, qall, qrows, keep, keep_lse,
    send1, recv1, send2, recv2, send3, recv3, final,
    k_sem, w_sem, qs_sem, qr_sem, s_sem, r_sem,
):
    requests, heads_here, width = q_ref.shape
    latent = wbuf.shape[1]
    devices = 4 * depth
    heads = devices * heads_here
    me = lax.axis_index("kv")
    core, row, level = lax.rem(me, 2), lax.rem(me // 2, 2), me // 4

    def device(dc, dr, dl):
        c = 1 - core if dc else core
        r = 1 - row if dr else row
        l = lax.rem(level + dl, depth) if dl else level
        return {"kv": (l * 2 + r) * 2 + c}

    def slot(dc, dr, dl):
        return (dc * 2 + dr) * depth + dl

    for r in range(requests):
        pltpu.make_async_copy(k_hbm.at[r], kbuf.at[r], k_sem.at[r]).start()
    pltpu.make_async_copy(w_hbm, wbuf, w_sem).start()

    core_peer, row_peer = device(1, 0, 0), device(0, 1, 0)
    level_peers = [device(0, 0, k) for k in range(1, depth)]
    barrier = pltpu.get_barrier_semaphore()
    for peer in [core_peer, row_peer] + level_peers:
        pl.semaphore_signal(barrier, inc=1, device_id=peer, device_id_type=MESH)
    pl.semaphore_wait(barrier, depth + 1)

    sends, arrivals = [], {}

    def send_query(src, place, peer):
        copy = pltpu.make_async_remote_copy(
            src_ref=src, dst_ref=qall.at[place],
            send_sem=qs_sem.at[place], recv_sem=qr_sem.at[place],
            device_id=peer, device_id_type=MESH,
        )
        copy.start()
        sends.append(copy)
        arrivals[place] = copy

    for k in range(1, depth):
        send_query(q_ref, slot(0, 0, (depth - k) % depth), level_peers[k - 1])
    send_query(q_ref, slot(0, 1, 0), row_peer)
    send_query(q_ref, slot(1, 0, 0), core_peer)
    qall[0] = q_ref[...]
    for k in range(1, depth):
        arrivals[slot(0, 0, k)].wait_recv()
        send_query(qall.at[slot(0, 0, k)], slot(0, 1, k), row_peer)
        send_query(qall.at[slot(0, 0, k)], slot(1, 0, k), core_peer)
    for k in range(depth):
        arrivals[slot(0, 1, k)].wait_recv()
        send_query(qall.at[slot(0, 1, k)], slot(1, 1, k), core_peer)
    for dr in range(2):
        for k in range(depth):
            arrivals[slot(1, dr, k)].wait_recv()

    def attend(r):
        for place in range(devices):
            qrows[place * heads_here : (place + 1) * heads_here, :] = qall[place, r].astype(jnp.float32)
        pltpu.make_async_copy(k_hbm.at[r], kbuf.at[r], k_sem.at[r]).wait()
        queries = qrows[...].astype(jnp.bfloat16)
        scores = lax.dot_general(
            queries, kbuf[r], (((1,), (1,)), ((), ())), preferred_element_type=jnp.float32
        )
        usable = pos_ref[r : r + 1, :] < len_ref[r]
        scores = jnp.where(usable, scores, masked_score)
        peak = jnp.max(scores, axis=1, keepdims=True)
        weights = jnp.exp((scores - peak) * softmax_scale)
        total = jnp.sum(weights, axis=1, keepdims=True)
        mixed = jnp.dot(
            weights.astype(jnp.bfloat16), kbuf[r, :, :latent], preferred_element_type=jnp.float32
        )
        return mixed * (1.0 / total), peak * softmax_scale + jnp.log(total)

    def send_part(src, dst, number, r, peer):
        copy = pltpu.make_async_remote_copy(
            src_ref=src, dst_ref=dst,
            send_sem=s_sem.at[number, r], recv_sem=r_sem.at[number, r],
            device_id=peer, device_id_type=MESH,
        )
        copy.start()
        sends.append(copy)
        return copy

    half, quarter = heads // 2, heads // 4
    first, second, third = {}, {}, {}

    def stage1(r):
        mixed, lse = attend(r)
        values, tail = packed(mixed[half:], lse[half:])
        send1[r, :, :latent] = values
        send1[r, :, latent:] = tail
        first[r] = send_part(send1.at[r], recv1.at[r], 0, r, core_peer)
        keep[r] = mixed[:half]
        keep_lse[r] = jnp.broadcast_to(lse[:half], (half, LANES))

    def stage2(r):
        first[r].wait_recv()
        mixed, lse = merge([(keep[r], keep_lse[r, :, 0:1]), unpacked(recv1.at[r], latent)])
        values, tail = packed(mixed[quarter:], lse[quarter:])
        send2[r, :, :latent] = values
        send2[r, :, latent:] = tail
        second[r] = send_part(send2.at[r], recv2.at[r], 1, r, row_peer)
        keep[r, :quarter] = mixed[:quarter]
        keep_lse[r, :quarter] = jnp.broadcast_to(lse[:quarter], (quarter, LANES))

    def stage3(r):
        second[r].wait_recv()
        mixed, lse = merge(
            [(keep[r, :quarter], keep_lse[r, :quarter, 0:1]), unpacked(recv2.at[r], latent)]
        )
        values, tail = packed(mixed, lse)
        for k in range(1, depth):
            rows = slice(k * heads_here, (k + 1) * heads_here)
            send3[r, k, :, :latent] = values[rows]
            send3[r, k, :, latent:] = tail[rows]
        for k in range(1, depth):
            third[r, k] = send_part(
                send3.at[r, k], recv3.at[r, depth - k], 1 + k, r, level_peers[k - 1]
            )
        keep[r, :heads_here] = mixed[:heads_here]
        keep_lse[r, :heads_here] = jnp.broadcast_to(lse[:heads_here], (heads_here, LANES))

    def stage4(r):
        parts = [(keep[r, :heads_here], keep_lse[r, :heads_here, 0:1])]
        for k in range(1, depth):
            third[r, k].wait_recv()
        for k in range(1, depth):
            parts.append(unpacked(recv3.at[r, k], latent))
        final[r] = merge(parts)[0]

    stages = [stage1, stage2, stage3, stage4]
    for step in range(requests + len(stages) - 1):
        for number, stage in enumerate(stages):
            if 0 <= step - number < requests:
                stage(step - number)

    pltpu.make_async_copy(w_hbm, wbuf, w_sem).wait()
    for h in range(heads_here):
        rows = final[:, h, :].astype(jnp.bfloat16)
        out_ref[:, h * wbuf.shape[2] : (h + 1) * wbuf.shape[2]] = jnp.dot(
            rows, wbuf[h], preferred_element_type=jnp.float32
        ).astype(out_ref.dtype)
    for copy in sends:
        copy.wait_send()


def shards(devices, absorbed_query, latent_cache, slot_position, context_lengths, value_up):
    depth = devices // 4
    requests, heads_here, width = absorbed_query.shape
    slots = latent_cache.shape[1]
    latent, value = value_up.shape[1:]
    heads = devices * heads_here
    wide = latent + LANES
    half, quarter = heads // 2, heads // 4
    vmem = pl.BlockSpec(memory_space=pltpu.VMEM)
    hbm = pl.BlockSpec(memory_space=pltpu.HBM)
    bf16, f32 = jnp.bfloat16, jnp.float32
    return pl.pallas_call(
        functools.partial(kernel, depth),
        out_shape=jax.ShapeDtypeStruct((requests, heads_here * value), bf16),
        in_specs=[vmem, hbm, vmem, pl.BlockSpec(memory_space=pltpu.SMEM), hbm],
        out_specs=vmem,
        scratch_shapes=[
            pltpu.VMEM((requests, slots, width), bf16),
            pltpu.VMEM(value_up.shape, bf16),
            pltpu.VMEM((devices, requests, heads_here, width), bf16),
            pltpu.VMEM((heads, width), f32),
            pltpu.VMEM((requests, half, latent), f32),
            pltpu.VMEM((requests, half, LANES), f32),
            pltpu.VMEM((requests, half, wide), bf16),
            pltpu.VMEM((requests, half, wide), bf16),
            pltpu.VMEM((requests, quarter, wide), bf16),
            pltpu.VMEM((requests, quarter, wide), bf16),
            pltpu.VMEM((requests, depth, heads_here, wide), bf16),
            pltpu.VMEM((requests, depth, heads_here, wide), bf16),
            pltpu.VMEM((requests, heads_here, latent), f32),
            pltpu.SemaphoreType.DMA((requests,)),
            pltpu.SemaphoreType.DMA,
            pltpu.SemaphoreType.DMA((devices,)),
            pltpu.SemaphoreType.DMA((devices,)),
            pltpu.SemaphoreType.DMA((1 + depth, requests)),
            pltpu.SemaphoreType.DMA((1 + depth, requests)),
        ],
        compiler_params=pltpu.CompilerParams(
            collective_id=0, has_side_effects=True, vmem_limit_bytes=56 * 1024 * 1024
        ),
        name="attention_step",
    )(absorbed_query, latent_cache, slot_position, context_lengths, value_up)


def solution(mesh):
    return jax.shard_map(
        functools.partial(shards, mesh.shape["kv"]),
        mesh=mesh,
        in_specs=(
            P("grp", "kv", None),
            P("grp", "kv", None),
            P("grp", "kv"),
            P("grp"),
            P("kv", None, None),
        ),
        out_specs=P("grp", "kv"),
        check_vma=False,
    )
```

```python
import functools

import jax
import jax.numpy as jnp
from jax import lax
from jax.experimental import pallas as pl
from jax.experimental.pallas import tpu as pltpu
from jax.sharding import PartitionSpec as P

softmax_scale = 192.0 ** (-0.5)
masked_score = -1e30
MESH = pl.DeviceIdType.MESH
LANES = 128


def merge(parts):
    peak = functools.reduce(jnp.maximum, [lse for _, lse in parts])
    factors = [jnp.exp(lse - peak) for _, lse in parts]
    total = sum(factors[1:], factors[0])
    inverse = 1.0 / total
    mixed = sum(
        [part * (f * inverse) for (part, _), f in zip(parts[1:], factors[1:])],
        parts[0][0] * (factors[0] * inverse),
    )
    return mixed, peak + jnp.log(total)


def packed(mixed, lse):
    lanes = lax.broadcasted_iota(jnp.int32, (mixed.shape[0], LANES), 1)
    high = lse.astype(jnp.bfloat16).astype(jnp.float32)
    rest = lse - high
    middle = rest.astype(jnp.bfloat16).astype(jnp.float32)
    low = rest - middle
    return mixed.astype(jnp.bfloat16), jnp.where(
        lanes == 0, high, jnp.where(lanes == 1, middle, low)
    ).astype(jnp.bfloat16)


def unpacked(ref, latent):
    mixed = ref[:, :latent].astype(jnp.float32)
    tail = ref[:, latent:].astype(jnp.float32)
    return mixed, (tail[:, 0:1] + tail[:, 1:2]) + tail[:, 2:3]


def kernel(
    depth, q_ref, k_hbm, pos_ref, len_ref, w_hbm, out_ref,
    kbuf, wbuf, qall, qrows, keep, keep_lse,
    send1, recv1, send2, recv2, send3, recv3, final,
    k_sem, w_sem, qs_sem, qr_sem, s_sem, r_sem,
):
    requests, heads_here, width = q_ref.shape
    latent = wbuf.shape[1]
    devices = 4 * depth
    heads = devices * heads_here
    me = lax.axis_index("kv")
    core, row, level = lax.rem(me, 2), lax.rem(me // 2, 2), me // 4

    def device(dc, dr, dl):
        c = 1 - core if dc else core
        r = 1 - row if dr else row
        l = lax.rem(level + dl, depth) if dl else level
        return {"kv": (l * 2 + r) * 2 + c}

    def slot(dc, dr, dl):
        return (dc * 2 + dr) * depth + dl

    for r in range(requests):
        pltpu.make_async_copy(k_hbm.at[r], kbuf.at[r], k_sem.at[r]).start()
    pltpu.make_async_copy(w_hbm, wbuf, w_sem).start()

    core_peer, row_peer = device(1, 0, 0), device(0, 1, 0)
    level_peers = [device(0, 0, k) for k in range(1, depth)]
    barrier = pltpu.get_barrier_semaphore()
    for peer in [core_peer, row_peer] + level_peers:
        pl.semaphore_signal(barrier, inc=1, device_id=peer, device_id_type=MESH)
    pl.semaphore_wait(barrier, depth + 1)

    sends, arrivals = [], {}

    def send_query(src, place, peer):
        copy = pltpu.make_async_remote_copy(
            src_ref=src, dst_ref=qall.at[place],
            send_sem=qs_sem.at[place], recv_sem=qr_sem.at[place],
            device_id=peer, device_id_type=MESH,
        )
        copy.start()
        sends.append(copy)
        arrivals[place] = copy

    for k in range(1, depth):
        send_query(q_ref, slot(0, 0, (depth - k) % depth), level_peers[k - 1])
    send_query(q_ref, slot(0, 1, 0), row_peer)
    send_query(q_ref, slot(1, 0, 0), core_peer)
    qall[0] = q_ref[...]
    for k in range(1, depth):
        arrivals[slot(0, 0, k)].wait_recv()
        send_query(qall.at[slot(0, 0, k)], slot(0, 1, k), row_peer)
        send_query(qall.at[slot(0, 0, k)], slot(1, 0, k), core_peer)
    for k in range(depth):
        arrivals[slot(0, 1, k)].wait_recv()
        send_query(qall.at[slot(0, 1, k)], slot(1, 1, k), core_peer)
    for dr in range(2):
        for k in range(depth):
            arrivals[slot(1, dr, k)].wait_recv()

    def attend(r):
        for place in range(devices):
            qrows[place * heads_here : (place + 1) * heads_here, :] = qall[place, r].astype(jnp.float32)
        pltpu.make_async_copy(k_hbm.at[r], kbuf.at[r], k_sem.at[r]).wait()
        queries = qrows[...].astype(jnp.bfloat16)
        scores = lax.dot_general(
            queries, kbuf[r], (((1,), (0,)), ((), ())), preferred_element_type=jnp.float32
        )
        usable = pos_ref[r : r + 1, :] < len_ref[r]
        scores = jnp.where(usable, scores, masked_score)
        peak = jnp.max(scores, axis=1, keepdims=True)
        weights = jnp.exp((scores - peak) * softmax_scale)
        total = jnp.sum(weights, axis=1, keepdims=True)
        mixed = lax.dot_general(
            weights.astype(jnp.bfloat16),
            kbuf[r, :latent, :],
            (((1,), (1,)), ((), ())),
            preferred_element_type=jnp.float32,
        )
        return mixed * (1.0 / total), peak * softmax_scale + jnp.log(total)

    def send_part(src, dst, number, r, peer):
        copy = pltpu.make_async_remote_copy(
            src_ref=src, dst_ref=dst,
            send_sem=s_sem.at[number, r], recv_sem=r_sem.at[number, r],
            device_id=peer, device_id_type=MESH,
        )
        copy.start()
        sends.append(copy)
        return copy

    half, quarter = heads // 2, heads // 4
    first, second, third = {}, {}, {}

    def stage1(r):
        mixed, lse = attend(r)
        values, tail = packed(mixed[half:], lse[half:])
        send1[r, :, :latent] = values
        send1[r, :, latent:] = tail
        first[r] = send_part(send1.at[r], recv1.at[r], 0, r, core_peer)
        keep[r] = mixed[:half]
        keep_lse[r] = jnp.broadcast_to(lse[:half], (half, LANES))

    def stage2(r):
        first[r].wait_recv()
        mixed, lse = merge([(keep[r], keep_lse[r, :, 0:1]), unpacked(recv1.at[r], latent)])
        values, tail = packed(mixed[quarter:], lse[quarter:])
        send2[r, :, :latent] = values
        send2[r, :, latent:] = tail
        second[r] = send_part(send2.at[r], recv2.at[r], 1, r, row_peer)
        keep[r, :quarter] = mixed[:quarter]
        keep_lse[r, :quarter] = jnp.broadcast_to(lse[:quarter], (quarter, LANES))

    def stage3(r):
        second[r].wait_recv()
        mixed, lse = merge(
            [(keep[r, :quarter], keep_lse[r, :quarter, 0:1]), unpacked(recv2.at[r], latent)]
        )
        values, tail = packed(mixed, lse)
        for k in range(1, depth):
            rows = slice(k * heads_here, (k + 1) * heads_here)
            send3[r, k, :, :latent] = values[rows]
            send3[r, k, :, latent:] = tail[rows]
        for k in range(1, depth):
            third[r, k] = send_part(
                send3.at[r, k], recv3.at[r, depth - k], 1 + k, r, level_peers[k - 1]
            )
        keep[r, :heads_here] = mixed[:heads_here]
        keep_lse[r, :heads_here] = jnp.broadcast_to(lse[:heads_here], (heads_here, LANES))

    def stage4(r):
        parts = [(keep[r, :heads_here], keep_lse[r, :heads_here, 0:1])]
        for k in range(1, depth):
            third[r, k].wait_recv()
        for k in range(1, depth):
            parts.append(unpacked(recv3.at[r, k], latent))
        final[r] = merge(parts)[0]

    stages = [stage1, stage2, stage3, stage4]
    for step in range(requests + len(stages) - 1):
        for number, stage in enumerate(stages):
            if 0 <= step - number < requests:
                stage(step - number)

    pltpu.make_async_copy(w_hbm, wbuf, w_sem).wait()
    for h in range(heads_here):
        rows = final[:, h, :].astype(jnp.bfloat16)
        out_ref[:, h * wbuf.shape[2] : (h + 1) * wbuf.shape[2]] = jnp.dot(
            rows, wbuf[h], preferred_element_type=jnp.float32
        ).astype(out_ref.dtype)
    for copy in sends:
        copy.wait_send()


def shards(devices, absorbed_query, latent_cache, slot_position, context_lengths, value_up):
    depth = devices // 4
    requests, heads_here, width = absorbed_query.shape
    slots = latent_cache.shape[1]
    latent, value = value_up.shape[1:]
    heads = devices * heads_here
    wide = latent + LANES
    half, quarter = heads // 2, heads // 4
    vmem = pl.BlockSpec(memory_space=pltpu.VMEM)
    hbm = pl.BlockSpec(memory_space=pltpu.HBM)
    bf16, f32 = jnp.bfloat16, jnp.float32
    return pl.pallas_call(
        functools.partial(kernel, depth),
        out_shape=jax.ShapeDtypeStruct((requests, heads_here * value), bf16),
        in_specs=[vmem, hbm, vmem, pl.BlockSpec(memory_space=pltpu.SMEM), hbm],
        out_specs=vmem,
        scratch_shapes=[
            pltpu.VMEM((requests, width, slots), bf16),
            pltpu.VMEM(value_up.shape, bf16),
            pltpu.VMEM((devices, requests, heads_here, width), bf16),
            pltpu.VMEM((heads, width), f32),
            pltpu.VMEM((requests, half, latent), f32),
            pltpu.VMEM((requests, half, LANES), f32),
            pltpu.VMEM((requests, half, wide), bf16),
            pltpu.VMEM((requests, half, wide), bf16),
            pltpu.VMEM((requests, quarter, wide), bf16),
            pltpu.VMEM((requests, quarter, wide), bf16),
            pltpu.VMEM((requests, depth, heads_here, wide), bf16),
            pltpu.VMEM((requests, depth, heads_here, wide), bf16),
            pltpu.VMEM((requests, heads_here, latent), f32),
            pltpu.SemaphoreType.DMA((requests,)),
            pltpu.SemaphoreType.DMA,
            pltpu.SemaphoreType.DMA((devices,)),
            pltpu.SemaphoreType.DMA((devices,)),
            pltpu.SemaphoreType.DMA((1 + depth, requests)),
            pltpu.SemaphoreType.DMA((1 + depth, requests)),
        ],
        compiler_params=pltpu.CompilerParams(
            collective_id=0, has_side_effects=True, vmem_limit_bytes=56 * 1024 * 1024
        ),
        name="attention_step",
    )(absorbed_query, jnp.swapaxes(latent_cache, 1, 2), slot_position, context_lengths, value_up)


def solution(mesh):
    return jax.shard_map(
        functools.partial(shards, mesh.shape["kv"]),
        mesh=mesh,
        in_specs=(
            P("grp", "kv", None),
            P("grp", "kv", None),
            P("grp", "kv"),
            P("grp"),
            P("kv", None, None),
        ),
        out_specs=P("grp", "kv"),
        check_vma=False,
    )
```

```python
import functools

import jax
import jax.numpy as jnp
from jax import lax
from jax.experimental import pallas as pl
from jax.experimental.pallas import tpu as pltpu
from jax.sharding import PartitionSpec as P

softmax_scale = 192.0 ** (-0.5)
masked_score = -1e30
MESH = pl.DeviceIdType.MESH
LANES = 128


def merge(parts):
    peak = functools.reduce(jnp.maximum, [lse for _, lse in parts])
    factors = [jnp.exp(lse - peak) for _, lse in parts]
    total = sum(factors[1:], factors[0])
    inverse = 1.0 / total
    mixed = sum(
        [part * (f * inverse) for (part, _), f in zip(parts[1:], factors[1:])],
        parts[0][0] * (factors[0] * inverse),
    )
    return mixed, peak + jnp.log(total)


def packed(mixed, lse):
    lanes = lax.broadcasted_iota(jnp.int32, (mixed.shape[0], LANES), 1)
    high = lse.astype(jnp.bfloat16).astype(jnp.float32)
    rest = lse - high
    middle = rest.astype(jnp.bfloat16).astype(jnp.float32)
    low = rest - middle
    return mixed.astype(jnp.bfloat16), jnp.where(
        lanes == 0, high, jnp.where(lanes == 1, middle, low)
    ).astype(jnp.bfloat16)


def unpacked(ref, latent):
    mixed = ref[:, :latent].astype(jnp.float32)
    tail = ref[:, latent:].astype(jnp.float32)
    return mixed, (tail[:, 0:1] + tail[:, 1:2]) + tail[:, 2:3]


def kernel(
    depth, q_ref, k_hbm, pos_ref, len_ref, w_hbm, out_ref,
    kbuf, wbuf, qall, qrows, keep, keep_lse,
    send1, recv1, send2, recv2, final,
    k_sem, w_sem, qs_sem, qr_sem, s_sem, r_sem,
):
    requests, heads_here, width = q_ref.shape
    latent = wbuf.shape[1]
    devices = 4 * depth
    heads = devices * heads_here
    me = lax.axis_index("kv")
    core, row, level = lax.rem(me, 2), lax.rem(me // 2, 2), me // 4

    def device(dc, dr, dl):
        c = 1 - core if dc else core
        r = 1 - row if dr else row
        l = lax.rem(level + dl, depth) if dl else level
        return {"kv": (l * 2 + r) * 2 + c}

    def slot(dc, dr, dl):
        return (dc * 2 + dr) * depth + dl

    for r in range(requests):
        pltpu.make_async_copy(k_hbm.at[r], kbuf.at[r], k_sem.at[r]).start()
    pltpu.make_async_copy(w_hbm, wbuf, w_sem).start()

    core_peer, row_peer = device(1, 0, 0), device(0, 1, 0)
    level_peers = {k: device(0, 0, k) for k in range(1, depth)}
    owners = {(dr, k): device(0, dr, k) for dr in range(2) for k in range(depth) if dr or k}
    barrier = pltpu.get_barrier_semaphore()
    for peer in [core_peer, row_peer] + list(level_peers.values()):
        pl.semaphore_signal(barrier, inc=1, device_id=peer, device_id_type=MESH)
    pl.semaphore_wait(barrier, depth + 1)

    sends, arrivals = [], {}

    def send_query(src, place, r, peer):
        copy = pltpu.make_async_remote_copy(
            src_ref=src.at[r], dst_ref=qall.at[place, r],
            send_sem=qs_sem.at[place, r], recv_sem=qr_sem.at[place, r],
            device_id=peer, device_id_type=MESH,
        )
        copy.start()
        sends.append(copy)
        arrivals[place, r] = copy

    def gather0(r):
        for k in range(1, depth):
            send_query(q_ref, slot(0, 0, depth - k), r, level_peers[k])
        send_query(q_ref, slot(0, 1, 0), r, row_peer)
        send_query(q_ref, slot(1, 0, 0), r, core_peer)

    def gather1(r):
        for k in range(1, depth):
            arrivals[slot(0, 0, k), r].wait_recv()
            send_query(qall.at[slot(0, 0, k)], slot(0, 1, k), r, row_peer)
            send_query(qall.at[slot(0, 0, k)], slot(1, 0, k), r, core_peer)

    def gather2(r):
        for k in range(depth):
            arrivals[slot(0, 1, k), r].wait_recv()
            send_query(qall.at[slot(0, 1, k)], slot(1, 1, k), r, core_peer)

    def gather3(r):
        for dr in range(2):
            for k in range(depth):
                arrivals[slot(1, dr, k), r].wait_recv()

    for r in range(requests):
        gather0(r)
    qall[0] = q_ref[...]

    def attend(r, between=None):
        for place in range(devices):
            qrows[place * heads_here : (place + 1) * heads_here, :] = qall[place, r].astype(jnp.float32)
        pltpu.make_async_copy(k_hbm.at[r], kbuf.at[r], k_sem.at[r]).wait()
        queries = qrows[...].astype(jnp.bfloat16)
        scores = lax.dot_general(
            queries, kbuf[r], (((1,), (0,)), ((), ())), preferred_element_type=jnp.float32
        )
        usable = pos_ref[r : r + 1, :] < len_ref[r]
        scores = jnp.where(usable, scores, masked_score)
        peak = jnp.max(scores, axis=1, keepdims=True)
        weights = jnp.exp((scores - peak) * softmax_scale)
        total = jnp.sum(weights, axis=1, keepdims=True)
        if between is not None:
            between()
        mixed = lax.dot_general(
            weights.astype(jnp.bfloat16),
            kbuf[r, :latent, :],
            (((1,), (1,)), ((), ())),
            preferred_element_type=jnp.float32,
        )
        return mixed * (1.0 / total), peak * softmax_scale + jnp.log(total)

    def send_part(src, dst, number, r, peer):
        copy = pltpu.make_async_remote_copy(
            src_ref=src, dst_ref=dst,
            send_sem=s_sem.at[number, r], recv_sem=r_sem.at[number, r],
            device_id=peer, device_id_type=MESH,
        )
        copy.start()
        sends.append(copy)
        return copy

    half = heads // 2
    first, second = {}, {}

    def reduce1(r):
        mixed, lse = attend(r, functools.partial(reduce2, r - 1) if r else None)
        values, tail = packed(mixed[half:], lse[half:])
        send1[r, :, :latent] = values
        send1[r, :, latent:] = tail
        first[r] = send_part(send1.at[r], recv1.at[r], 0, r, core_peer)
        keep[r] = mixed[:half]
        keep_lse[r] = jnp.broadcast_to(lse[:half], (half, LANES))

    def reduce2(r):
        first[r].wait_recv()
        mixed, lse = merge([(keep[r], keep_lse[r, :, 0:1]), unpacked(recv1.at[r], latent)])
        values, tail = packed(mixed, lse)
        for dr, k in owners:
            place = dr * depth + k
            rows = slice(place * heads_here, (place + 1) * heads_here)
            send2[r, place, :, :latent] = values[rows]
            send2[r, place, :, latent:] = tail[rows]
        for dr, k in owners:
            place, there = dr * depth + k, dr * depth + (depth - k) % depth
            second[r, there] = send_part(
                send2.at[r, place], recv2.at[r, there], there, r, owners[dr, k]
            )
        keep[r, :heads_here] = mixed[:heads_here]
        keep_lse[r, :heads_here] = jnp.broadcast_to(lse[:heads_here], (heads_here, LANES))

    def reduce3(r):
        parts = [(keep[r, :heads_here], keep_lse[r, :heads_here, 0:1])]
        for place in range(1, 2 * depth):
            second[r, place].wait_recv()
        for place in range(1, 2 * depth):
            parts.append(unpacked(recv2.at[r, place], latent))
        final[r] = merge(parts)[0]

    order = [(gather1, 0), (gather1, 1), (gather2, 0), (gather1, 2), (gather2, 1), (gather3, 0)]
    order = [item for item in order if item[1] < requests]
    for r in range(requests):
        order.append((reduce1, r))
        later = [(gather1, r + 3), (gather2, r + 2), (gather3, r + 1)]
        order += [item for item in later if item[1] < requests]
        if r > 1:
            order.append((reduce3, r - 2))
    order += [(reduce2, requests - 1)]
    order += [(reduce3, r) for r in range(max(requests - 2, 0), requests)]
    for stage, r in order:
        stage(r)

    pltpu.make_async_copy(w_hbm, wbuf, w_sem).wait()
    for h in range(heads_here):
        rows = final[:, h, :].astype(jnp.bfloat16)
        out_ref[:, h * wbuf.shape[2] : (h + 1) * wbuf.shape[2]] = jnp.dot(
            rows, wbuf[h], preferred_element_type=jnp.float32
        ).astype(out_ref.dtype)
    for copy in sends:
        copy.wait_send()


def shards(devices, absorbed_query, latent_cache, slot_position, context_lengths, value_up):
    depth = devices // 4
    requests, heads_here, width = absorbed_query.shape
    slots = latent_cache.shape[1]
    latent, value = value_up.shape[1:]
    heads = devices * heads_here
    wide = latent + LANES
    half = heads // 2
    vmem = pl.BlockSpec(memory_space=pltpu.VMEM)
    hbm = pl.BlockSpec(memory_space=pltpu.HBM)
    bf16, f32 = jnp.bfloat16, jnp.float32
    return pl.pallas_call(
        functools.partial(kernel, depth),
        out_shape=jax.ShapeDtypeStruct((requests, heads_here * value), bf16),
        in_specs=[vmem, hbm, vmem, pl.BlockSpec(memory_space=pltpu.SMEM), hbm],
        out_specs=vmem,
        scratch_shapes=[
            pltpu.VMEM((requests, width, slots), bf16),
            pltpu.VMEM(value_up.shape, bf16),
            pltpu.VMEM((devices, requests, heads_here, width), bf16),
            pltpu.VMEM((heads, width), f32),
            pltpu.VMEM((requests, half, latent), f32),
            pltpu.VMEM((requests, half, LANES), f32),
            pltpu.VMEM((requests, half, wide), bf16),
            pltpu.VMEM((requests, half, wide), bf16),
            pltpu.VMEM((requests, 2 * depth, heads_here, wide), bf16),
            pltpu.VMEM((requests, 2 * depth, heads_here, wide), bf16),
            pltpu.VMEM((requests, heads_here, latent), f32),
            pltpu.SemaphoreType.DMA((requests,)),
            pltpu.SemaphoreType.DMA,
            pltpu.SemaphoreType.DMA((devices, requests)),
            pltpu.SemaphoreType.DMA((devices, requests)),
            pltpu.SemaphoreType.DMA((2 * depth, requests)),
            pltpu.SemaphoreType.DMA((2 * depth, requests)),
        ],
        compiler_params=pltpu.CompilerParams(
            collective_id=0, has_side_effects=True, vmem_limit_bytes=56 * 1024 * 1024
        ),
        name="attention_step",
    )(absorbed_query, jnp.swapaxes(latent_cache, 1, 2), slot_position, context_lengths, value_up)


def solution(mesh):
    return jax.shard_map(
        functools.partial(shards, mesh.shape["kv"]),
        mesh=mesh,
        in_specs=(
            P("grp", "kv", None),
            P("grp", "kv", None),
            P("grp", "kv"),
            P("grp"),
            P("kv", None, None),
        ),
        out_specs=P("grp", "kv"),
        check_vma=False,
    )
```

```python
import functools

import jax
import jax.numpy as jnp
from jax import lax
from jax.experimental import pallas as pl
from jax.experimental.pallas import tpu as pltpu
from jax.sharding import PartitionSpec as P

softmax_scale = 192.0 ** (-0.5)
masked_score = -1e30
MESH = pl.DeviceIdType.MESH
LANES = 128


def merge(parts):
    peak = functools.reduce(jnp.maximum, [lse for _, lse in parts])
    factors = [jnp.exp(lse - peak) for _, lse in parts]
    total = sum(factors[1:], factors[0])
    inverse = 1.0 / total
    mixed = sum(
        [part * (f * inverse) for (part, _), f in zip(parts[1:], factors[1:])],
        parts[0][0] * (factors[0] * inverse),
    )
    return mixed, peak + jnp.log(total)


def packed(mixed, lse):
    lanes = lax.broadcasted_iota(jnp.int32, (mixed.shape[0], LANES), 1)
    high = lse.astype(jnp.bfloat16).astype(jnp.float32)
    rest = lse - high
    middle = rest.astype(jnp.bfloat16).astype(jnp.float32)
    low = rest - middle
    return mixed.astype(jnp.bfloat16), jnp.where(
        lanes == 0, high, jnp.where(lanes == 1, middle, low)
    ).astype(jnp.bfloat16)


def unpacked(ref, latent):
    mixed = ref[:, :latent].astype(jnp.float32)
    tail = ref[:, latent:].astype(jnp.float32)
    return mixed, (tail[:, 0:1] + tail[:, 1:2]) + tail[:, 2:3]


def kernel(
    depth, q_ref, k_hbm, pos_ref, len_ref, w_hbm, out_ref,
    kbuf, wbuf, qall, qrows, keep, keep_lse,
    send1, recv1, send2, recv2, final,
    k_sem, w_sem, qs_sem, qr_sem, s_sem, r_sem,
):
    requests, heads_here, width = q_ref.shape
    latent = wbuf.shape[1]
    devices = 4 * depth
    heads = devices * heads_here
    me = lax.axis_index("kv")
    core, row, level = lax.rem(me, 2), lax.rem(me // 2, 2), me // 4

    def device(dc, dr, dl):
        c = 1 - core if dc else core
        r = 1 - row if dr else row
        l = lax.rem(level + dl, depth) if dl else level
        return {"kv": (l * 2 + r) * 2 + c}

    def slot(dc, dr, dl):
        return (dc * 2 + dr) * depth + dl

    for r in range(requests):
        pltpu.make_async_copy(k_hbm.at[r], kbuf.at[r], k_sem.at[r]).start()
    pltpu.make_async_copy(w_hbm, wbuf, w_sem).start()

    core_peer, row_peer = device(1, 0, 0), device(0, 1, 0)
    level_peers = {k: device(0, 0, k) for k in range(1, depth)}
    owners = {(dr, k): device(0, dr, k) for dr in range(2) for k in range(depth) if dr or k}
    barrier = pltpu.get_barrier_semaphore()
    for peer in [core_peer, row_peer] + list(level_peers.values()):
        pl.semaphore_signal(barrier, inc=1, device_id=peer, device_id_type=MESH)
    pl.semaphore_wait(barrier, depth + 1)

    sends, arrivals = [], {}

    def send_query(src, place, r, peer):
        copy = pltpu.make_async_remote_copy(
            src_ref=src.at[r], dst_ref=qall.at[place, r],
            send_sem=qs_sem.at[place, r], recv_sem=qr_sem.at[place, r],
            device_id=peer, device_id_type=MESH,
        )
        copy.start()
        sends.append(copy)
        arrivals[place, r] = copy

    def gather0(r):
        for k in range(1, depth):
            send_query(q_ref, slot(0, 0, depth - k), r, level_peers[k])
        send_query(q_ref, slot(0, 1, 0), r, row_peer)
        send_query(q_ref, slot(1, 0, 0), r, core_peer)

    def gather1(r):
        for k in range(1, depth):
            arrivals[slot(0, 0, k), r].wait_recv()
            send_query(qall.at[slot(0, 0, k)], slot(0, 1, k), r, row_peer)
            send_query(qall.at[slot(0, 0, k)], slot(1, 0, k), r, core_peer)

    def gather2(r):
        for k in range(depth):
            arrivals[slot(0, 1, k), r].wait_recv()
            send_query(qall.at[slot(0, 1, k)], slot(1, 1, k), r, core_peer)

    def gather3(r):
        for dr in range(2):
            for k in range(depth):
                arrivals[slot(1, dr, k), r].wait_recv()

    for r in range(requests):
        gather0(r)
    qall[0] = q_ref[...]

    def attend(r, between=None):
        for place in range(devices):
            qrows[place * heads_here : (place + 1) * heads_here, :] = qall[place, r].astype(jnp.float32)
        pltpu.make_async_copy(k_hbm.at[r], kbuf.at[r], k_sem.at[r]).wait()
        queries = qrows[...].astype(jnp.bfloat16)
        scores = lax.dot_general(
            queries, kbuf[r], (((1,), (0,)), ((), ())), preferred_element_type=jnp.float32
        )
        usable = pos_ref[r : r + 1, :] < len_ref[r]
        scores = jnp.where(usable, scores, masked_score)
        peak = jnp.max(scores, axis=1, keepdims=True)
        weights = jnp.exp((scores - peak) * softmax_scale)
        total = jnp.sum(weights, axis=1, keepdims=True)
        if between is not None:
            between()
        mixed = lax.dot_general(
            weights.astype(jnp.bfloat16),
            kbuf[r, :latent, :],
            (((1,), (1,)), ((), ())),
            preferred_element_type=jnp.float32,
        )
        return mixed * (1.0 / total), peak * softmax_scale + jnp.log(total)

    def send_part(src, dst, number, r, peer):
        copy = pltpu.make_async_remote_copy(
            src_ref=src, dst_ref=dst,
            send_sem=s_sem.at[number, r], recv_sem=r_sem.at[number, r],
            device_id=peer, device_id_type=MESH,
        )
        copy.start()
        sends.append(copy)
        return copy

    half = heads // 2
    first, second = {}, {}

    def reduce1(r):
        mixed, lse = attend(r, functools.partial(reduce2, r - 1) if r else None)
        values, tail = packed(mixed[half:], lse[half:])
        send1[r, :, :latent] = values
        send1[r, :, latent:] = tail
        first[r] = send_part(send1.at[r], recv1.at[r], 0, r, core_peer)
        keep[r] = mixed[:half]
        keep_lse[r] = jnp.broadcast_to(lse[:half], (half, LANES))

    def reduce2(r):
        first[r].wait_recv()
        mixed, lse = merge([(keep[r], keep_lse[r, :, 0:1]), unpacked(recv1.at[r], latent)])
        values, tail = packed(mixed, lse)
        for dr, k in owners:
            place = dr * depth + k
            rows = slice(place * heads_here, (place + 1) * heads_here)
            send2[r, place, :, :latent] = values[rows]
            send2[r, place, :, latent:] = tail[rows]
        for dr, k in sorted(owners, key=lambda o: -(o[0] + min(o[1], depth - o[1]))):
            place, there = dr * depth + k, dr * depth + (depth - k) % depth
            second[r, there] = send_part(
                send2.at[r, place], recv2.at[r, there], there, r, owners[dr, k]
            )
        keep[r, :heads_here] = mixed[:heads_here]
        keep_lse[r, :heads_here] = jnp.broadcast_to(lse[:heads_here], (heads_here, LANES))

    def reduce3(r):
        parts = [(keep[r, :heads_here], keep_lse[r, :heads_here, 0:1])]
        for place in range(1, 2 * depth):
            second[r, place].wait_recv()
        for place in range(1, 2 * depth):
            parts.append(unpacked(recv2.at[r, place], latent))
        final[r] = merge(parts)[0]

    order = [(gather1, 0), (gather1, 1), (gather2, 0), (gather1, 2), (gather2, 1), (gather3, 0)]
    order = [item for item in order if item[1] < requests]
    for r in range(requests):
        order.append((reduce1, r))
        later = [(gather1, r + 3), (gather2, r + 2), (gather3, r + 1)]
        order += [item for item in later if item[1] < requests]
        if r > 1:
            order.append((reduce3, r - 2))
    order += [(reduce2, requests - 1)]
    order += [(reduce3, r) for r in range(max(requests - 2, 0), requests)]
    for stage, r in order:
        stage(r)

    pltpu.make_async_copy(w_hbm, wbuf, w_sem).wait()
    for h in range(heads_here):
        rows = final[:, h, :].astype(jnp.bfloat16)
        out_ref[:, h * wbuf.shape[2] : (h + 1) * wbuf.shape[2]] = jnp.dot(
            rows, wbuf[h], preferred_element_type=jnp.float32
        ).astype(out_ref.dtype)
    for copy in sends:
        copy.wait_send()


def shards(devices, absorbed_query, latent_cache, slot_position, context_lengths, value_up):
    depth = devices // 4
    requests, heads_here, width = absorbed_query.shape
    slots = latent_cache.shape[1]
    latent, value = value_up.shape[1:]
    heads = devices * heads_here
    wide = latent + LANES
    half = heads // 2
    vmem = pl.BlockSpec(memory_space=pltpu.VMEM)
    hbm = pl.BlockSpec(memory_space=pltpu.HBM)
    bf16, f32 = jnp.bfloat16, jnp.float32
    return pl.pallas_call(
        functools.partial(kernel, depth),
        out_shape=jax.ShapeDtypeStruct((requests, heads_here * value), bf16),
        in_specs=[vmem, hbm, vmem, pl.BlockSpec(memory_space=pltpu.SMEM), hbm],
        out_specs=vmem,
        scratch_shapes=[
            pltpu.VMEM((requests, width, slots), bf16),
            pltpu.VMEM(value_up.shape, bf16),
            pltpu.VMEM((devices, requests, heads_here, width), bf16),
            pltpu.VMEM((heads, width), f32),
            pltpu.VMEM((requests, half, latent), f32),
            pltpu.VMEM((requests, half, LANES), f32),
            pltpu.VMEM((requests, half, wide), bf16),
            pltpu.VMEM((requests, half, wide), bf16),
            pltpu.VMEM((requests, 2 * depth, heads_here, wide), bf16),
            pltpu.VMEM((requests, 2 * depth, heads_here, wide), bf16),
            pltpu.VMEM((requests, heads_here, latent), f32),
            pltpu.SemaphoreType.DMA((requests,)),
            pltpu.SemaphoreType.DMA,
            pltpu.SemaphoreType.DMA((devices, requests)),
            pltpu.SemaphoreType.DMA((devices, requests)),
            pltpu.SemaphoreType.DMA((2 * depth, requests)),
            pltpu.SemaphoreType.DMA((2 * depth, requests)),
        ],
        compiler_params=pltpu.CompilerParams(
            collective_id=0, has_side_effects=True, vmem_limit_bytes=56 * 1024 * 1024
        ),
        name="attention_step",
    )(absorbed_query, jnp.swapaxes(latent_cache, 1, 2), slot_position, context_lengths, value_up)


def solution(mesh):
    return jax.shard_map(
        functools.partial(shards, mesh.shape["kv"]),
        mesh=mesh,
        in_specs=(
            P("grp", "kv", None),
            P("grp", "kv", None),
            P("grp", "kv"),
            P("grp"),
            P("kv", None, None),
        ),
        out_specs=P("grp", "kv"),
        check_vma=False,
    )
```
